512 devices in a mesh: seg: 16 (over z), sec: 32 (over y, x, core).
Axes of the slice: x: 4, y: 4, z: 16, core: 2. Of those that a mesh axis runs over, the one named last changes fastest.
Arguments:
- boundary_env: bfloat16 [16, 32, 13, 256, 256], P('seg', 'sec'), may hold values from -6 to 6
- site_block_tensors: bfloat16 [32, 32, 4, 256, 256], P('seg', 'sec'), may hold values from -0.375 to 0.375
- mpo_tensors: bfloat16 [32, 4, 13, 13], P('seg'), may hold values from -1.75 to 1.75
- block_mask: int32 [32, 32, 4], P('seg', 'sec'), may hold values 0 or 1
- sector_dims: int32 [32], replicated, may hold values from 128 to 256, as said below
Outputs:
- handed_env: bfloat16 [16, 32, 13, 256, 256], P('seg', 'sec')
The draws below stay inside these ranges and needn't reach their ends.
Inputs may be any that keep to these rules, and one draw needn't show every extreme that they name: `sector_dims`: each entry is 128 or 256, and both occur in every draw.
All inputs are finite; a program needn't handle non-finite values. No bound on the sum of `block_mask` on one device may be relied on, other than what follows from the above.
Results may differ from the reference program's by a relative error of at most 0.02.
Values may be sent and summed in bfloat16 or wider, within the bound.
A program may use at most 64 MiB of HBM per device.

```python
import jax
import jax.numpy as jnp
from jax import lax

WB = 13
CAP = 256
ND = 4
SITES = 2
NSEG = 16
NSEC = 32
CHAIN_SITES = 32


def draw_sector_dims(key, part):
    keys = jax.random.split(key, 3)
    coin_flips = jax.random.randint(keys[0], (NSEC,), 0, 2)
    big_slot = jax.random.randint(keys[1], (), 0, NSEC)
    small_slot = (big_slot + 1 + jax.random.randint(keys[2], (), 0, NSEC - 1)) % NSEC
    coin_flips = coin_flips.at[big_slot].set(1).at[small_slot].set(0)
    return (CAP // 2 * (1 + coin_flips)).astype(jnp.int32)


def plant(drawn, key, low, largest):
    index_at = [jax.random.randint(jax.random.fold_in(key, axis), (), 0, length) for axis, length in enumerate(drawn.shape)]
    main_axis = drawn.shape.index(max(drawn.shape))
    next_to = index_at[:main_axis] + [(index_at[main_axis] + 1) % drawn.shape[main_axis]] + index_at[main_axis + 1:]
    return drawn.at[tuple(index_at)].set(low).at[tuple(next_to)].set(largest)


def level_of(key, shape, cuts, smallest, high):
    def one(position, shards_of):
        draws = jax.random.uniform(jax.random.fold_in(jax.random.fold_in(key, 6), position), (shards_of,), jnp.float32, smallest / len(cuts), high / len(cuts))
        return jnp.repeat(jnp.exp(draws), shape[position] // shards_of).reshape((-1,) + (1,) * (len(shape) - position - 1))

    factor_of = one(*cuts[0])
    for cut in cuts[1:]:
        factor_of = factor_of * one(*cut)
    return factor_of


def scatter_about(stream_key, dims, scale, limit, pieces=(), dtype=jnp.bfloat16):
    values = scale * jax.random.normal(stream_key, dims, jnp.float32)
    if pieces:
        values = values * level_of(stream_key, dims, pieces, -0.22, 0.18)
    return jnp.clip(values, -limit, limit).astype(dtype)


def setup_inputs(seed: int = 0) -> dict:
    key_list = jax.random.split(jax.random.key(seed), 6)
    return {
        "boundary_env": scatter_about(key_list[0], (NSEG, NSEC, WB, CAP, CAP), 1.0, 6.0, ((0, 16), (1, 32))),
        "site_block_tensors": scatter_about(key_list[1], (CHAIN_SITES, NSEC, 4, CAP, CAP), CAP ** -0.5, 0.375, ((0, 16), (1, 32))),
        "mpo_tensors": scatter_about(key_list[2], (CHAIN_SITES, 4, WB, WB), WB ** -0.5, 1.75, ((0, 16),)),
        "block_mask": plant((jax.random.randint(key_list[3], (CHAIN_SITES, NSEC, 4), 0, 4) < 3).astype(jnp.int32), jax.random.fold_in(key_list[3], 1), 0, 1),
        "sector_dims": draw_sector_dims(jax.random.fold_in(key_list[5], 71), 0),
    }


def sector_tables(sector_dims):
    sectors = jnp.arange(NSEC)
    offsets = jnp.array([0, ND, 1, ND + 1])
    down_step = jnp.array([0, 0, 1, 1])
    targets = sectors[:, None] + offsets[None, :]
    allowed = (targets < NSEC) & ((down_step[None, :] == 0) | ((sectors % ND)[:, None] < ND - 1))
    target_dims = jnp.where(allowed, sector_dims[jnp.clip(targets, 0, NSEC - 1)], 0)
    line = jnp.arange(CAP)
    row_live = line[None, :] < sector_dims[:, None]
    col_live = line[None, None, :] < target_dims[:, :, None]
    return allowed, row_live, col_live


def sector_update(left_environ_tensor, block_list, weight_factors):
    output_collection = []
    for carry_state in range(4):
        merged_mixture = jnp.einsum('umi,ue->emi', left_environ_tensor.astype(jnp.float32), weight_factors[carry_state].astype(jnp.float32)).astype(jnp.bfloat16)
        combined_mixture = jnp.einsum('gip,pq->giq', merged_mixture.astype(jnp.float32), block_list[carry_state].astype(jnp.float32)).astype(jnp.bfloat16)
        output_collection.append(jnp.einsum('ba,vbc->vac', block_list[carry_state].astype(jnp.float32), combined_mixture.astype(jnp.float32)).astype(jnp.bfloat16))
    return jnp.stack(output_collection)


def move_up(values, steps):
    filler = jnp.zeros((steps,) + values.shape[1:], jnp.float32)
    return jnp.concatenate([filler, values[:-steps].astype(jnp.float32)], axis=0)


def reference(boundary_env, site_block_tensors, mpo_tensors, block_mask, sector_dims):
    allowed, row_live, col_live = sector_tables(sector_dims)
    env_live = (row_live[:, None, :, None] & row_live[:, None, None, :]).astype(jnp.bfloat16)

    def one_segment(segment):
        left_environ_tensor = boundary_env[segment] * env_live
        for site_pos in range(SITES):
            chain_pos = segment * SITES + site_pos
            present = block_mask[chain_pos] * allowed.astype(jnp.int32)
            factor = present[:, :, None, None] * row_live[:, None, :, None].astype(jnp.int32) * col_live[:, :, None, :].astype(jnp.int32)
            block_list = site_block_tensors[chain_pos] * factor.astype(jnp.bfloat16)
            weight_factors = mpo_tensors[chain_pos]
            partial_value = lax.map(lambda pair: sector_update(pair[0], pair[1], weight_factors), (left_environ_tensor, block_list))
            total = partial_value[:, 0].astype(jnp.float32) + move_up(partial_value[:, 1], ND)
            total = total + move_up(partial_value[:, 2], 1) + move_up(partial_value[:, 3], ND + 1)
            left_environ_tensor = total.astype(jnp.bfloat16)
        return left_environ_tensor

    finals = lax.map(one_segment, jnp.arange(NSEG).astype(jnp.int32))
    return jnp.concatenate([jnp.zeros_like(finals[:1]), finals[:-1]], axis=0)
```

```python
import functools

import jax
import jax.numpy as jnp
from jax import lax
from jax.experimental import pallas as pl
from jax.experimental.pallas import tpu as pltpu
from jax.sharding import PartitionSpec as P

ND = 4
ROWS = 16
MESH = pl.DeviceIdType.MESH
F32 = jnp.float32
BF16 = jnp.bfloat16


def kernel(
    nseg, nsec,
    env_ref, blk_ref, mpo_ref, mask_ref, dims_ref,
    out_ref,
    kron, bm, bt, mixed, env2, acc, c_snd, d_snd, h_snd, c_in, d_in, h_in, z_snd,
    c_ss, c_rs, d_ss, d_rs, h_ss, h_rs, z_ss, z_rs,
):
    sites, wb, cap = blk_ref.shape[0], env_ref.shape[0], env_ref.shape[-1]
    seg = lax.axis_index("seg")
    q = lax.axis_index("sec")
    j = lax.rem(q, ND)
    has_c_out = q < nsec - ND
    has_c_in = q >= ND
    has_d_out = j < ND - 1
    has_d_in = j > 0
    even = lax.rem(j, 2) == 0
    mid = j == 1
    h_near_out = even & has_c_out
    h_far_out = mid & has_c_out
    h_out = h_near_out | h_far_out
    h_near_in = jnp.logical_not(even) & has_c_out
    h_far_in = (j == 2) & (q >= ND + 1)
    z_out = seg < nseg - 1
    z_in = seg > 0

    def at(s, t):
        return (s, t)

    up = lax.rem(q + ND, nsec)
    down = lax.rem(q + nsec - ND, nsec)
    nxt = lax.rem(q + 1, nsec)
    prv = lax.rem(q + nsec - 1, nsec)
    far = lax.rem(q + ND + 1, nsec)
    far_back = lax.rem(q + nsec - ND - 1, nsec)
    h_target = jnp.where(mid, far, nxt)
    after = lax.rem(seg + 1, nseg)
    before = lax.rem(seg + nseg - 1, nseg)

    barrier = pltpu.get_barrier_semaphore()
    met = jnp.int32(0)
    for cond, s, t in (
        (has_c_out, seg, up), (has_c_in, seg, down), (has_d_out, seg, nxt), (has_d_in, seg, prv),
        (h_far_out, seg, far), (h_far_in, seg, far_back), (z_out, after, q), (z_in, before, q),
    ):
        @pl.when(cond)
        def _():
            pl.semaphore_signal(barrier, inc=1, device_id=at(s, t), device_id_type=MESH)
        met = met + cond.astype(jnp.int32)

    own = dims_ref[q]
    offsets = (0, ND, 1, ND + 1)
    row = lax.broadcasted_iota(jnp.int32, (cap, cap), 0)
    col = lax.broadcasted_iota(jnp.int32, (cap, cap), 1)
    for n in range(sites):
        for s in range(4):
            ok = q + offsets[s] < nsec
            if s >= 2:
                ok = ok & has_d_out
            target = dims_ref[jnp.where(ok, q + offsets[s], 0)]
            width = target * ok.astype(jnp.int32) * mask_ref[n, s]
            live = jnp.where((row < own) & (col < width), 1.0, 0.0)
            b = blk_ref[n, s].astype(F32) * live
            bm[n, s] = b.astype(BF16)
            bt[n, s] = b.T.astype(BF16)

    span = wb * ROWS
    pick = (lax.broadcasted_iota(jnp.int32, (span, wb), 0) // ROWS == lax.broadcasted_iota(jnp.int32, (span, wb), 1))
    pick = jnp.where(pick, 1.0, 0.0).astype(BF16)
    diag = (
        lax.rem(lax.broadcasted_iota(jnp.int32, (span, span), 0), ROWS)
        == lax.rem(lax.broadcasted_iota(jnp.int32, (span, span), 1), ROWS)
    )
    for n in range(sites):
        for s in range(4):
            left = lax.dot_general(pick, mpo_ref[n, s], (((1,), (1,)), ((), ())), preferred_element_type=F32)
            both = lax.dot_general(left.astype(BF16), pick, (((1,), (1,)), ((), ())), preferred_element_type=F32)
            kron[n, pl.ds(s * span, span), :] = jnp.where(diag, both, 0.0).astype(BF16)

    def mix(n, first):
        def one(h, carry):
            rows = pl.ds(pl.multiple_of(h * ROWS, ROWS), ROWS)
            slab = (env_ref if first else env2)[:, rows, :].reshape(span, cap)
            if first:
                r = h * ROWS + lax.rem(lax.broadcasted_iota(jnp.int32, (span, cap), 0), ROWS)
                c = lax.broadcasted_iota(jnp.int32, (span, cap), 1)
                slab = jnp.where((r < own) & (c < own), slab.astype(F32), 0.0).astype(BF16)
            for s in range(4):
                got = jnp.dot(kron[n, pl.ds(s * span, span), :], slab, preferred_element_type=F32)
                mixed[s, :, rows, :] = got.astype(BF16).reshape(wb, ROWS, cap)
            return carry
        lax.fori_loop(0, cap // ROWS, one, 0)

    def product(n, s, v):
        blended = jnp.dot(mixed[s, v], bm[n, s], preferred_element_type=F32).astype(BF16)
        return jnp.dot(bt[n, s], blended, preferred_element_type=F32)

    def c_copy(n, v):
        return pltpu.make_async_remote_copy(
            src_ref=c_snd.at[n, v], dst_ref=c_in.at[n, v], send_sem=c_ss.at[n, v], recv_sem=c_rs.at[n, v],
            device_id=at(seg, up), device_id_type=MESH)

    def d_copy(n, v):
        return pltpu.make_async_remote_copy(
            src_ref=d_snd.at[n, v], dst_ref=d_in.at[n, v], send_sem=d_ss.at[n, v], recv_sem=d_rs.at[n, v],
            device_id=at(seg, nxt), device_id_type=MESH)

    def h_copy(n, v):
        return pltpu.make_async_remote_copy(
            src_ref=h_snd.at[n, v], dst_ref=h_in.at[n, v], send_sem=h_ss.at[n, v], recv_sem=h_rs.at[n, v],
            device_id=at(seg, h_target), device_id_type=MESH)

    def z_copy(v):
        return pltpu.make_async_remote_copy(
            src_ref=z_snd.at[v], dst_ref=out_ref.at[v], send_sem=z_ss.at[v], recv_sem=z_rs.at[v],
            device_id=at(after, q), device_id_type=MESH)

    def site(n, last):
        mix(n, n == 0)

        if n == 0:
            pl.semaphore_wait(barrier, met)

        def outgoing(v, carry):
            @pl.when(h_out)
            def _():
                h_snd[n, v] = product(n, 3, v).astype(BF16)
                h_copy(n, v).start()

            @pl.when(has_d_out)
            def _():
                d_snd[n, v] = product(n, 2, v).astype(BF16)
                d_copy(n, v).start()

            @pl.when(has_c_out)
            def _():
                acc[v] = product(n, 1, v)

                @pl.when(h_near_in)
                def _():
                    h_copy(n, v).wait_recv()
                    acc[v] = acc[v] + h_in[n, v].astype(F32)

                c_snd[n, v] = acc[v].astype(BF16)
                c_copy(n, v).start()
            return carry

        lax.fori_loop(0, wb, outgoing, 0)

        def staying(v, carry):
            acc[v] = product(n, 0, v)
            return carry

        lax.fori_loop(0, wb, staying, 0)

        def finish(v, carry):
            total = acc[v]
            acc[v] = total

            @pl.when(has_d_in)
            def _():
                d_copy(n, v).wait_recv()
                acc[v] = acc[v] + d_in[n, v].astype(F32)

            @pl.when(h_far_in)
            def _():
                h_copy(n, v).wait_recv()
                acc[v] = acc[v] + h_in[n, v].astype(F32)

            @pl.when(has_c_in)
            def _():
                c_copy(n, v).wait_recv()
                acc[v] = acc[v] + c_in[n, v].astype(F32)

            if last:
                @pl.when(z_out)
                def _():
                    z_snd[v] = acc[v].astype(BF16)
                    z_copy(v).start()
            else:
                env2[v] = acc[v].astype(BF16)
            return carry

        lax.fori_loop(0, wb, finish, 0)

    for n in range(sites):
        site(n, n == sites - 1)

    @pl.when(jnp.logical_not(z_in))
    def _():
        out_ref[...] = jnp.zeros_like(out_ref)

    def drain(v, carry):
        for n in range(sites):
            @pl.when(h_out)
            def _():
                h_copy(n, v).wait_send()

            @pl.when(has_d_out)
            def _():
                d_copy(n, v).wait_send()

            @pl.when(has_c_out)
            def _():
                c_copy(n, v).wait_send()

        @pl.when(z_out)
        def _():
            z_copy(v).wait_send()

        @pl.when(z_in)
        def _():
            z_copy(v).wait_recv()
        return carry

    lax.fori_loop(0, wb, drain, 0)


def solution(mesh):
    nseg, nsec = mesh.shape["seg"], mesh.shape["sec"]

    def body(boundary_env, site_block_tensors, mpo_tensors, block_mask, sector_dims):
        env = boundary_env[0, 0]
        blocks = site_block_tensors[:, 0]
        masks = block_mask[:, 0]
        sites, wb, cap = blocks.shape[0], env.shape[0], env.shape[-1]
        span = wb * ROWS
        vmem = pl.BlockSpec(memory_space=pltpu.VMEM)
        smem = pl.BlockSpec(memory_space=pltpu.SMEM)
        stream = pltpu.VMEM((sites, wb, cap, cap), BF16)
        sems = pltpu.SemaphoreType.DMA((sites, wb))
        out = pl.pallas_call(
            functools.partial(kernel, nseg, nsec),
            out_shape=jax.ShapeDtypeStruct(env.shape, BF16),
            in_specs=[vmem, vmem, vmem, smem, smem],
            out_specs=vmem,
            scratch_shapes=[
                pltpu.VMEM((sites, 4 * span, span), BF16),
                pltpu.VMEM((sites, 4, cap, cap), BF16),
                pltpu.VMEM((sites, 4, cap, cap), BF16),
                pltpu.VMEM((4, wb, cap, cap), BF16),
                pltpu.VMEM((wb, cap, cap), BF16),
                pltpu.VMEM((wb, cap, cap), F32),
                stream, stream, stream, stream, stream, stream,
                pltpu.VMEM((wb, cap, cap), BF16),
                sems, sems, sems, sems, sems, sems,
                pltpu.SemaphoreType.DMA((wb,)),
                pltpu.SemaphoreType.DMA((wb,)),
            ],
            compiler_params=pltpu.CompilerParams(
                collective_id=0, has_side_effects=True, vmem_limit_bytes=60 * 1024 * 1024),
        )(env, blocks, mpo_tensors, masks, sector_dims)
        return out[None, None]

    in_specs = (
        P("seg", "sec", None, None, None),
        P("seg", "sec", None, None, None),
        P("seg", None, None, None),
        P("seg", "sec", None),
        P(),
    )
    return jax.shard_map(
        body, mesh=mesh, in_specs=in_specs, out_specs=P("seg", "sec", None, None, None), check_vma=False)
```

```python
import functools

import jax
import jax.numpy as jnp
from jax import lax
from jax.experimental import pallas as pl
from jax.experimental.pallas import tpu as pltpu
from jax.sharding import PartitionSpec as P

ND = 4
ROWS = 16
CHUNK = 32
UNROLL = 4
MESH = pl.DeviceIdType.MESH
F32 = jnp.float32
BF16 = jnp.bfloat16


def dot(a, b):
    return jnp.dot(a, b, preferred_element_type=F32)


def each(count, step, body):
    def trip(k, carry):
        for u in range(step):
            body(k * step + u)
        return carry
    lax.fori_loop(0, count // step, trip, 0)
    for i in range(count // step * step, count):
        body(i)


def kernel(
    nseg, nsec,
    env_ref, blk_ref, mpo_ref, mask_ref, dims_ref,
    out_ref,
    kron, live, bm, bp, to_a, to_c, half_a, half_c, acc, prev1, env2, prev2, c1_snd, c1_in, rel, c2_snd, c2_in, z_snd,
    e_ss, e_rs, b_ss, b_rs, c1_ss, c1_rs, rel_ss, rel_rs, fwd_ss, f_ss, f_rs, c2_ss, c2_rs, z_ss, z_rs, ready,
):
    sites, wb, cap = blk_ref.shape[0], env_ref.shape[0], env_ref.shape[-1]
    span = wb * ROWS
    pieces = cap // CHUNK
    seg = lax.axis_index("seg")
    q = lax.axis_index("sec")
    j = lax.rem(q, ND)
    place = lax.rem(q, 2 * ND)
    has_up = q < nsec - ND
    has_down = q >= ND
    has_next = j < ND - 1
    has_prev = j > 0
    z_out = seg < nseg - 1
    z_in = seg > 0

    up = lax.rem(q + ND, nsec)
    down = lax.rem(q + nsec - ND, nsec)
    nxt = lax.rem(q + 1, nsec)
    prv = lax.rem(q + nsec - 1, nsec)
    after = lax.rem(seg + 1, nseg)
    before = lax.rem(seg + nseg - 1, nseg)

    through = (j == 0) & has_up
    relay = jnp.where(place == 0, q + 7, q - 1)
    relay = lax.rem(relay + nsec, nsec)
    served = jnp.where(place == 7, q - 7, q + 1)
    relays = (j == ND - 1) & (served < nsec - ND)
    served = lax.rem(served + nsec, nsec)
    onward = lax.rem(served + ND, nsec)
    via = (j == 0) & has_down
    via_from = lax.rem(jnp.where(place == 4, q + 3, q - 5) + nsec, nsec)

    barrier = pltpu.get_barrier_semaphore()
    met = jnp.int32(0)
    for cond, s, t in (
        (has_up, seg, up), (has_down, seg, down), (has_next, seg, nxt), (has_prev, seg, prv),
        (z_out, after, q), (z_in, before, q), (through, seg, relay), (relays, seg, served),
        (relays, seg, onward), (via, seg, via_from),
    ):
        @pl.when(cond)
        def _():
            pl.semaphore_signal(barrier, inc=1, device_id=(s, t), device_id_type=MESH)
        met = met + cond.astype(jnp.int32)

    def remote(src, dst, ss, rs, s, t):
        return pltpu.make_async_remote_copy(
            src_ref=src, dst_ref=dst, send_sem=ss, recv_sem=rs, device_id=(s, t), device_id_type=MESH)

    def rows_of(h):
        return pl.ds(pl.multiple_of(h * CHUNK, CHUNK), CHUNK)

    def e_copy():
        return remote(env_ref, prev1, e_ss, e_rs, seg, nxt)

    def b_copy(n):
        return remote(bm.at[n, pl.ds(2, 2)], bp.at[n], b_ss.at[n], b_rs.at[n], seg, nxt)

    def c1_copy(h):
        return remote(c1_snd.at[:, rows_of(h)], c1_in.at[:, rows_of(h)], c1_ss.at[h], c1_rs.at[h], seg, up)

    def rel_copy(h):
        return remote(c1_snd.at[:, rows_of(h)], rel.at[:, rows_of(h)], rel_ss.at[h], rel_rs.at[h], seg, relay)

    def fwd_copy(h):
        return remote(rel.at[:, rows_of(h)], c1_in.at[:, rows_of(h)], fwd_ss.at[h], c1_rs.at[h], seg, onward)

    def f_copy(h):
        return remote(env2.at[:, rows_of(h)], prev2.at[:, rows_of(h)], f_ss.at[h], f_rs.at[h], seg, nxt)

    def c2_copy(v):
        return remote(c2_snd.at[v], c2_in.at[v], c2_ss.at[v], c2_rs.at[v], seg, up)

    def z_copy(v):
        return remote(z_snd.at[v], out_ref.at[v], z_ss.at[v], z_rs.at[v], after, q)

    own = dims_ref[q]
    before_own = dims_ref[prv]
    row = lax.broadcasted_iota(jnp.int32, (cap, cap), 0)
    col = lax.broadcasted_iota(jnp.int32, (cap, cap), 1)

    def build_kron(n):
        pick = lax.broadcasted_iota(jnp.int32, (span, wb), 0) // ROWS == lax.broadcasted_iota(jnp.int32, (span, wb), 1)
        pick = jnp.where(pick, 1.0, 0.0).astype(BF16)
        diag = (
            lax.rem(lax.broadcasted_iota(jnp.int32, (span, span), 0), ROWS)
            == lax.rem(lax.broadcasted_iota(jnp.int32, (span, span), 1), ROWS)
        )
        mpo = mpo_ref[n].astype(F32)
        for s in range(4):
            left = lax.dot_general(pick, mpo[:, s, :].astype(BF16), (((1,), (1,)), ((), ())), preferred_element_type=F32)
            both = lax.dot_general(left.astype(BF16), pick, (((1,), (1,)), ((), ())), preferred_element_type=F32)
            kron[n, pl.ds(s * span, span), :] = jnp.where(diag, both, 0.0).astype(BF16)

    def trim(n, s):
        ahead = (0, ND, 1, ND + 1)[s]
        ok = q + ahead < nsec
        if s >= 2:
            ok = ok & has_next
        width = dims_ref[jnp.where(ok, q + ahead, 0)] * ok.astype(jnp.int32) * mask_ref[n, s]
        b = blk_ref[n, s].astype(F32) * jnp.where((row < own) & (col < width), 1.0, 0.0)
        bm[n, s] = b.astype(BF16)
        if s == 0:
            to_a[n, :, pl.ds(0, cap)] = b.T.astype(BF16)
        if s == 1:
            to_c[n, :, pl.ds(0, cap)] = b.T.astype(BF16)

    def turn_prev(n):
        to_a[n, :, pl.ds(cap, cap)] = bp[n, 0].astype(F32).T.astype(BF16)
        to_c[n, :, pl.ds(cap, cap)] = bp[n, 1].astype(F32).T.astype(BF16)

    def front(n, h, source, first, block_a, block_c, limit):
        mixed = []
        for k in range(CHUNK // ROWS):
            rows = pl.ds(pl.multiple_of(h * CHUNK + k * ROWS, ROWS), ROWS)
            slab = source[:, rows, :]
            if limit is not None:
                slab = slab * live[limit, rows, :][None]
            mixed.append(dot(kron[n, pl.ds(2 * first * span, 2 * span), :], slab.reshape(span, cap)).astype(BF16))
        for half, block, s in ((half_a, block_a, 0), (half_c, block_c, 1)):
            stacked = jnp.concatenate([m[s * span:(s + 1) * span] for m in mixed], axis=0)
            got = dot(stacked, block).astype(BF16)
            for k in range(CHUNK // ROWS):
                rows = pl.ds(pl.multiple_of(first * cap + h * CHUNK + k * ROWS, ROWS), ROWS)
                half[:, rows, :] = got[k * span:(k + 1) * span].reshape(wb, ROWS, cap)

    def front_own(n, h):
        front(n, h, env2 if n else env_ref, 0, bm[n, 0], bm[n, 1], None if n else 0)

    def front_prev(n, h):
        front(n, h, prev2 if n else prev1, 1, bp[n, 0], bp[n, 1], None if n else 1)

    build_kron(0)
    pl.semaphore_wait(barrier, met)

    @pl.when(has_next)
    def _():
        e_copy().start()

    trim(0, 2)
    trim(0, 3)

    @pl.when(has_next)
    def _():
        b_copy(0).start()

    trim(0, 0)
    trim(0, 1)
    live[0] = jnp.where((row < own) & (col < own), 1.0, 0.0).astype(BF16)
    live[1] = jnp.where((row < before_own) & (col < before_own), 1.0, 0.0).astype(BF16)
    each(pieces, 2, lambda h: front_own(0, h))

    @pl.when(has_prev)
    def _():
        b_copy(0).wait_recv()
        turn_prev(0)
        e_copy().wait_recv()
        each(pieces, 2, lambda h: front_prev(0, h))

    @pl.when(jnp.logical_not(has_prev))
    def _():
        for half in (half_a, half_c):
            half[:, pl.ds(cap, cap), :] = jnp.zeros((wb, cap, cap), BF16)
        for to in (to_a, to_c):
            for n in range(sites):
                to[n, :, pl.ds(cap, cap)] = jnp.zeros((cap, cap), BF16)

    @pl.when(has_up)
    def _():
        def one(v):
            c1_snd[v] = dot(to_c[0], half_c[v]).astype(BF16)
        each(wb, UNROLL, one)

        @pl.when(through)
        def _():
            each(pieces, 1, lambda h: rel_copy(h).start())

        @pl.when(jnp.logical_not(through))
        def _():
            each(pieces, 1, lambda h: c1_copy(h).start())

    for s in (2, 3, 0, 1):
        trim(1, s)

    @pl.when(has_next)
    def _():
        b_copy(1).start()

    build_kron(1)

    @pl.when(has_prev)
    def _():
        b_copy(1).wait_recv()
        turn_prev(1)

    def keep(n):
        def one(v):
            acc[v] = dot(to_a[n], half_a[v])
        each(wb, UNROLL, one)

    keep(0)

    both = (j == 1) | (j == 2)

    def arrive(h):
        @pl.when(relays)
        def _():
            rel_copy(h).wait_recv()
            fwd_copy(h).start()

        rows = rows_of(h)

        @pl.when(has_down)
        def _():
            c1_copy(h).wait_recv()
            env2[:, rows, :] = (acc[:, rows, :] + c1_in[:, rows, :].astype(F32)).astype(BF16)

        @pl.when(jnp.logical_not(has_down))
        def _():
            env2[:, rows, :] = acc[:, rows, :].astype(BF16)

        @pl.when(has_next)
        def _():
            f_copy(h).start()

        front_own(1, h)

        @pl.when(both & (h > 0))
        def _():
            f_copy(h - 1).wait_recv()
            front_prev(1, h - 1)

    each(pieces, 1, arrive)

    @pl.when(has_down)
    def _():
        pl.semaphore_signal(ready, inc=1, device_id=(seg, down), device_id_type=MESH)

    @pl.when(both)
    def _():
        f_copy(pieces - 1).wait_recv()
        front_prev(1, pieces - 1)

    @pl.when(j == ND - 1)
    def _():
        def one(h):
            f_copy(h).wait_recv()
            front_prev(1, h)
        each(pieces, 1, one)

    @pl.when(has_up)
    def _():
        pl.semaphore_wait(ready, 1)

        def one(v):
            c2_snd[v] = dot(to_c[1], half_c[v]).astype(BF16)
            c2_copy(v).start()
        each(wb, UNROLL, one)

    keep(1)

    def last(v):
        @pl.when(has_down)
        def _():
            c2_copy(v).wait_recv()
            acc[v] = acc[v] + c2_in[v].astype(F32)

        @pl.when(z_out)
        def _():
            z_snd[v] = acc[v].astype(BF16)
            z_copy(v).start()

    each(wb, 1, last)

    @pl.when(jnp.logical_not(z_in))
    def _():
        out_ref[...] = jnp.zeros_like(out_ref)

    @pl.when(has_next)
    def _():
        e_copy().wait_send()
        for n in range(sites):
            b_copy(n).wait_send()
        each(pieces, 1, lambda h: f_copy(h).wait_send())

    @pl.when(through)
    def _():
        each(pieces, 1, lambda h: rel_copy(h).wait_send())

    @pl.when(has_up & jnp.logical_not(through))
    def _():
        each(pieces, 1, lambda h: c1_copy(h).wait_send())

    @pl.when(relays)
    def _():
        each(pieces, 1, lambda h: fwd_copy(h).wait_send())

    @pl.when(has_up)
    def _():
        each(wb, 1, lambda v: c2_copy(v).wait_send())

    @pl.when(z_out)
    def _():
        each(wb, 1, lambda v: z_copy(v).wait_send())

    @pl.when(z_in)
    def _():
        each(wb, 1, lambda v: z_copy(v).wait_recv())


def solution(mesh):
    nseg, nsec = mesh.shape["seg"], mesh.shape["sec"]

    def body(boundary_env, site_block_tensors, mpo_tensors, block_mask, sector_dims):
        env = boundary_env[0, 0]
        blocks = site_block_tensors[:, 0]
        masks = block_mask[:, 0]
        sites, wb, cap = blocks.shape[0], env.shape[0], env.shape[-1]
        span = wb * ROWS
        pieces = cap // CHUNK
        vmem = pl.BlockSpec(memory_space=pltpu.VMEM)
        smem = pl.BlockSpec(memory_space=pltpu.SMEM)
        whole = pltpu.VMEM((wb, cap, cap), BF16)
        half = pltpu.VMEM((wb, 2 * cap, cap), BF16)
        to = pltpu.VMEM((sites, cap, 2 * cap), BF16)
        one = pltpu.SemaphoreType.DMA
        by_site = pltpu.SemaphoreType.DMA((sites,))
        by_piece = pltpu.SemaphoreType.DMA((pieces,))
        by_channel = pltpu.SemaphoreType.DMA((wb,))
        out = pl.pallas_call(
            functools.partial(kernel, nseg, nsec),
            out_shape=jax.ShapeDtypeStruct(env.shape, BF16),
            in_specs=[vmem, vmem, vmem, smem, smem],
            out_specs=vmem,
            scratch_shapes=[
                pltpu.VMEM((sites, 4 * span, span), BF16),
                pltpu.VMEM((2, cap, cap), BF16),
                pltpu.VMEM((sites, 4, cap, cap), BF16),
                pltpu.VMEM((sites, 2, cap, cap), BF16),
                to, to, half, half,
                pltpu.VMEM((wb, cap, cap), F32),
                whole, whole, whole, whole, whole, whole, whole, whole, whole,
                one, one, by_site, by_site, by_piece, by_piece, by_piece, by_piece, by_piece, by_piece, by_piece,
                by_channel, by_channel, by_channel, by_channel,
                pltpu.SemaphoreType.REGULAR,
            ],
            compiler_params=pltpu.CompilerParams(
                collective_id=0, has_side_effects=True, vmem_limit_bytes=60 * 1024 * 1024),
        )(env, blocks, jnp.swapaxes(mpo_tensors, 1, 2), masks, sector_dims)
        return jnp.where(lax.axis_index("seg") > 0, out, 0)[None, None]

    in_specs = (
        P("seg", "sec", None, None, None),
        P("seg", "sec", None, None, None),
        P("seg", None, None, None),
        P("seg", "sec", None),
        P(),
    )
    return jax.shard_map(
        body, mesh=mesh, in_specs=in_specs, out_specs=P("seg", "sec", None, None, None), check_vma=False)
```

```python
import functools

import jax
import jax.numpy as jnp
from jax import lax
from jax.experimental import pallas as pl
from jax.experimental.pallas import tpu as pltpu
from jax.sharding import PartitionSpec as P

ND = 4
ROWS = 16
CHUNK = 32
RELAYED = 8
UNROLL = 4
MESH = pl.DeviceIdType.MESH
F32 = jnp.float32
BF16 = jnp.bfloat16


def dot(a, b):
    return jnp.dot(a, b, preferred_element_type=F32)


def each(count, step, body):
    def trip(k, carry):
        for u in range(step):
            body(k * step + u)
        return carry
    lax.fori_loop(0, count // step, trip, 0)
    for i in range(count // step * step, count):
        body(i)


def kernel(
    nseg, nsec,
    env_ref, blk_ref, mpo_ref, mask_ref, dims_ref,
    out_ref,
    kron, live, bm, bp, to_a, to_c, half_a, half_c, acc, prev1, env2, prev2, c1_snd, c1_in, rel, c2_snd, c2_in, z_snd,
    e_ss, e_rs, b_ss, b_rs, c1_ss, c1_rs, rel_ss, rel_rs, fwd_ss, f_ss, f_rs, c2_ss, c2_rs, z_ss, z_rs, ready,
):
    sites, wb, cap = blk_ref.shape[0], env_ref.shape[0], env_ref.shape[-1]
    span = wb * ROWS
    pieces = cap // CHUNK
    seg = lax.axis_index("seg")
    q = lax.axis_index("sec")
    j = lax.rem(q, ND)
    place = lax.rem(q, 2 * ND)
    has_up = q < nsec - ND
    has_down = q >= ND
    has_next = j < ND - 1
    has_prev = j > 0
    z_out = seg < nseg - 1
    z_in = seg > 0

    up = lax.rem(q + ND, nsec)
    down = lax.rem(q + nsec - ND, nsec)
    nxt = lax.rem(q + 1, nsec)
    prv = lax.rem(q + nsec - 1, nsec)
    after = lax.rem(seg + 1, nseg)
    before = lax.rem(seg + nseg - 1, nseg)

    through = (j == 0) & has_up
    relay = jnp.where(place == 0, q + 7, q - 1)
    relay = lax.rem(relay + nsec, nsec)
    served = jnp.where(place == 7, q - 7, q + 1)
    relays = (j == ND - 1) & (served < nsec - ND)
    served = lax.rem(served + nsec, nsec)
    onward = lax.rem(served + ND, nsec)
    via = (j == 0) & has_down
    via_from = lax.rem(jnp.where(place == 4, q + 3, q - 5) + nsec, nsec)

    barrier = pltpu.get_barrier_semaphore()
    met = jnp.int32(0)
    for cond, s, t in (
        (has_up, seg, up), (has_down, seg, down), (has_next, seg, nxt), (has_prev, seg, prv),
        (z_out, after, q), (z_in, before, q), (through, seg, relay), (relays, seg, served),
        (relays, seg, onward), (via, seg, via_from),
    ):
        @pl.when(cond)
        def _():
            pl.semaphore_signal(barrier, inc=1, device_id=(s, t), device_id_type=MESH)
        met = met + cond.astype(jnp.int32)

    def remote(src, dst, ss, rs, s, t):
        return pltpu.make_async_remote_copy(
            src_ref=src, dst_ref=dst, send_sem=ss, recv_sem=rs, device_id=(s, t), device_id_type=MESH)

    def rows_of(h):
        return pl.ds(pl.multiple_of(h * CHUNK, CHUNK), CHUNK)

    def e_copy():
        return remote(env_ref, prev1, e_ss, e_rs, seg, nxt)

    def b_copy(n):
        return remote(bm.at[n, pl.ds(2, 2)], bp.at[n], b_ss.at[n], b_rs.at[n], seg, nxt)

    def c1_copy(h):
        return remote(c1_snd.at[:, rows_of(h)], c1_in.at[:, rows_of(h)], c1_ss.at[h], c1_rs.at[h], seg, up)

    def rel_copy(h):
        return remote(c1_snd.at[:, rows_of(h)], rel.at[:, rows_of(h)], rel_ss.at[h], rel_rs.at[h], seg, relay)

    def fwd_copy(h):
        return remote(rel.at[:, rows_of(h)], c1_in.at[:, rows_of(h)], fwd_ss.at[h], c1_rs.at[h], seg, onward)

    def f_copy(h):
        return remote(env2.at[:, rows_of(h)], prev2.at[:, rows_of(h)], f_ss.at[h], f_rs.at[h], seg, nxt)

    def c2_copy(v):
        return remote(c2_snd.at[v], c2_in.at[v], c2_ss.at[v], c2_rs.at[v], seg, up)

    def z_copy(v):
        return remote(z_snd.at[v], out_ref.at[v], z_ss.at[v], z_rs.at[v], after, q)

    own = dims_ref[q]
    before_own = dims_ref[prv]
    row = lax.broadcasted_iota(jnp.int32, (cap, cap), 0)
    col = lax.broadcasted_iota(jnp.int32, (cap, cap), 1)

    def build_kron(n):
        pick = lax.broadcasted_iota(jnp.int32, (span, wb), 0) // ROWS == lax.broadcasted_iota(jnp.int32, (span, wb), 1)
        pick = jnp.where(pick, 1.0, 0.0).astype(BF16)
        diag = (
            lax.rem(lax.broadcasted_iota(jnp.int32, (span, span), 0), ROWS)
            == lax.rem(lax.broadcasted_iota(jnp.int32, (span, span), 1), ROWS)
        )
        mpo = mpo_ref[n].astype(F32)
        for s in range(4):
            left = lax.dot_general(pick, mpo[:, s, :].astype(BF16), (((1,), (1,)), ((), ())), preferred_element_type=F32)
            both = lax.dot_general(left.astype(BF16), pick, (((1,), (1,)), ((), ())), preferred_element_type=F32)
            kron[n, pl.ds(s * span, span), :] = jnp.where(diag, both, 0.0).astype(BF16)

    def trim(n, s):
        ahead = (0, ND, 1, ND + 1)[s]
        ok = q + ahead < nsec
        if s >= 2:
            ok = ok & has_next
        width = dims_ref[jnp.where(ok, q + ahead, 0)] * ok.astype(jnp.int32) * mask_ref[n, s]
        b = blk_ref[n, s].astype(F32) * jnp.where((row < own) & (col < width), 1.0, 0.0)
        bm[n, s] = b.astype(BF16)
        if s == 0:
            to_a[n, :, pl.ds(0, cap)] = b.T.astype(BF16)
        if s == 1:
            to_c[n, :, pl.ds(0, cap)] = b.T.astype(BF16)

    def turn_prev(n):
        to_a[n, :, pl.ds(cap, cap)] = bp[n, 0].astype(F32).T.astype(BF16)
        to_c[n, :, pl.ds(cap, cap)] = bp[n, 1].astype(F32).T.astype(BF16)

    def front(n, h, source, first, blocks, limit, states):
        mixed = []
        for k in range(CHUNK // ROWS):
            rows = pl.ds(pl.multiple_of(h * CHUNK + k * ROWS, ROWS), ROWS)
            slab = source[:, rows, :]
            if limit is not None:
                slab = slab * live[limit, rows, :][None]
            weights = kron[n, pl.ds((2 * first + states[0]) * span, len(states) * span), :]
            mixed.append(dot(weights, slab.reshape(span, cap)).astype(BF16))
        for i, s in enumerate(states):
            half = (half_a, half_c)[s]
            stacked = jnp.concatenate([m[i * span:(i + 1) * span] for m in mixed], axis=0)
            got = dot(stacked, blocks[s]).astype(BF16)
            for k in range(CHUNK // ROWS):
                rows = pl.ds(pl.multiple_of(first * cap + h * CHUNK + k * ROWS, ROWS), ROWS)
                half[:, rows, :] = got[k * span:(k + 1) * span].reshape(wb, ROWS, cap)

    def front_own(n, h, states=(0, 1)):
        front(n, h, env2 if n else env_ref, 0, bm.at[n], None if n else 0, states)

    def front_prev(n, h, states=(0, 1)):
        front(n, h, prev2 if n else prev1, 1, bp.at[n], None if n else 1, states)

    build_kron(0)
    pl.semaphore_wait(barrier, met)

    @pl.when(has_next)
    def _():
        e_copy().start()

    trim(0, 2)
    trim(0, 3)

    @pl.when(has_next)
    def _():
        b_copy(0).start()

    trim(0, 0)
    trim(0, 1)
    live[0] = jnp.where((row < own) & (col < own), 1.0, 0.0).astype(BF16)
    live[1] = jnp.where((row < before_own) & (col < before_own), 1.0, 0.0).astype(BF16)
    each(pieces, 4, lambda h: front_own(0, h, (1,)))

    @pl.when(has_prev)
    def _():
        b_copy(0).wait_recv()
        turn_prev(0)
        e_copy().wait_recv()
        each(pieces, 4, lambda h: front_prev(0, h, (1,)))

    @pl.when(jnp.logical_not(has_prev))
    def _():
        for half in (half_a, half_c):
            half[:, pl.ds(cap, cap), :] = jnp.zeros((wb, cap, cap), BF16)
        for to in (to_a, to_c):
            for n in range(sites):
                to[n, :, pl.ds(cap, cap)] = jnp.zeros((cap, cap), BF16)

    @pl.when(has_up)
    def _():
        def one(v):
            c1_snd[v] = dot(to_c[0], half_c[v]).astype(BF16)
        each(wb, UNROLL, one)

        @pl.when(through)
        def _():
            each(RELAYED, 1, lambda h: rel_copy(h).start())
            each(pieces - RELAYED, 1, lambda h: c1_copy(h + RELAYED).start())

        @pl.when(jnp.logical_not(through))
        def _():
            each(pieces, 1, lambda h: c1_copy(h).start())

    for s in (2, 3, 0, 1):
        trim(1, s)

    @pl.when(has_next)
    def _():
        b_copy(1).start()

    build_kron(1)

    @pl.when(has_prev)
    def _():
        b_copy(1).wait_recv()
        turn_prev(1)

    each(pieces, 4, lambda h: front_own(0, h, (0,)))

    @pl.when(has_prev)
    def _():
        each(pieces, 4, lambda h: front_prev(0, h, (0,)))

    def keep(n):
        def one(v):
            acc[v] = dot(to_a[n], half_a[v])
        each(wb, UNROLL, one)

    keep(0)

    both = (j == 1) | (j == 2)

    def arrive(h):
        @pl.when(relays & (h < RELAYED))
        def _():
            rel_copy(h).wait_recv()
            fwd_copy(h).start()

        rows = rows_of(h)

        @pl.when(has_down)
        def _():
            c1_copy(h).wait_recv()
            env2[:, rows, :] = (acc[:, rows, :] + c1_in[:, rows, :].astype(F32)).astype(BF16)

        @pl.when(jnp.logical_not(has_down))
        def _():
            env2[:, rows, :] = acc[:, rows, :].astype(BF16)

        @pl.when(has_next)
        def _():
            f_copy(h).start()

        front_own(1, h)

        @pl.when(both & (h > 0))
        def _():
            f_copy(h - 1).wait_recv()
            front_prev(1, h - 1)

    each(pieces, 1, arrive)

    @pl.when(has_down)
    def _():
        pl.semaphore_signal(ready, inc=1, device_id=(seg, down), device_id_type=MESH)

    @pl.when(both)
    def _():
        f_copy(pieces - 1).wait_recv()
        front_prev(1, pieces - 1)

    @pl.when(j == ND - 1)
    def _():
        def one(h):
            f_copy(h).wait_recv()
            front_prev(1, h)
        each(pieces, 1, one)

    @pl.when(has_up)
    def _():
        pl.semaphore_wait(ready, 1)

        def one(v):
            c2_snd[v] = dot(to_c[1], half_c[v]).astype(BF16)
            c2_copy(v).start()
        each(wb, UNROLL, one)

    keep(1)

    def last(v):
        @pl.when(has_down)
        def _():
            c2_copy(v).wait_recv()
            acc[v] = acc[v] + c2_in[v].astype(F32)

        @pl.when(z_out)
        def _():
            z_snd[v] = acc[v].astype(BF16)
            z_copy(v).start()

    each(wb, 1, last)

    @pl.when(jnp.logical_not(z_in))
    def _():
        out_ref[...] = jnp.zeros_like(out_ref)

    @pl.when(has_next)
    def _():
        e_copy().wait_send()
        for n in range(sites):
            b_copy(n).wait_send()
        each(pieces, 1, lambda h: f_copy(h).wait_send())

    @pl.when(through)
    def _():
        each(RELAYED, 1, lambda h: rel_copy(h).wait_send())
        each(pieces - RELAYED, 1, lambda h: c1_copy(h + RELAYED).wait_send())

    @pl.when(has_up & jnp.logical_not(through))
    def _():
        each(pieces, 1, lambda h: c1_copy(h).wait_send())

    @pl.when(relays)
    def _():
        each(RELAYED, 1, lambda h: fwd_copy(h).wait_send())

    @pl.when(has_up)
    def _():
        each(wb, 1, lambda v: c2_copy(v).wait_send())

    @pl.when(z_out)
    def _():
        each(wb, 1, lambda v: z_copy(v).wait_send())

    @pl.when(z_in)
    def _():
        each(wb, 1, lambda v: z_copy(v).wait_recv())


def solution(mesh):
    nseg, nsec = mesh.shape["seg"], mesh.shape["sec"]

    def body(boundary_env, site_block_tensors, mpo_tensors, block_mask, sector_dims):
        env = boundary_env[0, 0]
        blocks = site_block_tensors[:, 0]
        masks = block_mask[:, 0]
        sites, wb, cap = blocks.shape[0], env.shape[0], env.shape[-1]
        span = wb * ROWS
        pieces = cap // CHUNK
        vmem = pl.BlockSpec(memory_space=pltpu.VMEM)
        smem = pl.BlockSpec(memory_space=pltpu.SMEM)
        whole = pltpu.VMEM((wb, cap, cap), BF16)
        half = pltpu.VMEM((wb, 2 * cap, cap), BF16)
        to = pltpu.VMEM((sites, cap, 2 * cap), BF16)
        one = pltpu.SemaphoreType.DMA
        by_site = pltpu.SemaphoreType.DMA((sites,))
        by_piece = pltpu.SemaphoreType.DMA((pieces,))
        by_channel = pltpu.SemaphoreType.DMA((wb,))
        out = pl.pallas_call(
            functools.partial(kernel, nseg, nsec),
            out_shape=jax.ShapeDtypeStruct(env.shape, BF16),
            in_specs=[vmem, vmem, vmem, smem, smem],
            out_specs=vmem,
            scratch_shapes=[
                pltpu.VMEM((sites, 4 * span, span), BF16),
                pltpu.VMEM((2, cap, cap), BF16),
                pltpu.VMEM((sites, 4, cap, cap), BF16),
                pltpu.VMEM((sites, 2, cap, cap), BF16),
                to, to, half, half,
                pltpu.VMEM((wb, cap, cap), F32),
                whole, whole, whole, whole, whole, whole, whole, whole, whole,
                one, one, by_site, by_site, by_piece, by_piece, by_piece, by_piece, by_piece, by_piece, by_piece,
                by_channel, by_channel, by_channel, by_channel,
                pltpu.SemaphoreType.REGULAR,
            ],
            compiler_params=pltpu.CompilerParams(
                collective_id=0, has_side_effects=True, vmem_limit_bytes=60 * 1024 * 1024),
        )(env, blocks, jnp.swapaxes(mpo_tensors, 1, 2), masks, sector_dims)
        return jnp.where(lax.axis_index("seg") > 0, out, 0)[None, None]

    in_specs = (
        P("seg", "sec", None, None, None),
        P("seg", "sec", None, None, None),
        P("seg", None, None, None),
        P("seg", "sec", None),
        P(),
    )
    return jax.shard_map(
        body, mesh=mesh, in_specs=in_specs, out_specs=P("seg", "sec", None, None, None), check_vma=False)
```

```python
import functools

import jax
import jax.numpy as jnp
from jax import lax
from jax.experimental import pallas as pl
from jax.experimental.pallas import tpu as pltpu
from jax.sharding import PartitionSpec as P

ND = 4
ROWS = 16
CHUNK = 32
RELAYED = 8
UNROLL = 4
MESH = pl.DeviceIdType.MESH
F32 = jnp.float32
BF16 = jnp.bfloat16


def dot(a, b):
    return jnp.dot(a, b, preferred_element_type=F32)


def each(count, step, body):
    def trip(k, carry):
        for u in range(step):
            body(k * step + u)
        return carry
    lax.fori_loop(0, count // step, trip, 0)
    for i in range(count // step * step, count):
        body(i)


def kernel(
    nseg, nsec,
    env_ref, blk_ref, mpo_ref, mask_ref, dims_ref,
    out_ref,
    kron, live, bm, bp, to_a, to_c, half_a, half_c, acc, prev1, env2, prev2, c1_snd, c1_in, rel, c2_snd, c2_in, z_snd,
    e_ss, e_rs, b_ss, b_rs, c1_ss, c1_rs, rel_ss, rel_rs, fwd_ss, f_ss, f_rs, c2_ss, c2_rs, z_ss, z_rs, ready,
):
    sites, wb, cap = blk_ref.shape[0], env_ref.shape[0], env_ref.shape[-1]
    span = wb * ROWS
    pieces = cap // CHUNK
    seg = lax.axis_index("seg")
    q = lax.axis_index("sec")
    j = lax.rem(q, ND)
    place = lax.rem(q, 2 * ND)
    has_up = q < nsec - ND
    has_down = q >= ND
    has_next = j < ND - 1
    has_prev = j > 0
    z_out = seg < nseg - 1
    z_in = seg > 0

    up = lax.rem(q + ND, nsec)
    down = lax.rem(q + nsec - ND, nsec)
    nxt = lax.rem(q + 1, nsec)
    prv = lax.rem(q + nsec - 1, nsec)
    after = lax.rem(seg + 1, nseg)
    before = lax.rem(seg + nseg - 1, nseg)

    through = (j == 0) & has_up
    relay = jnp.where(place == 0, q + 7, q - 1)
    relay = lax.rem(relay + nsec, nsec)
    served = jnp.where(place == 7, q - 7, q + 1)
    relays = (j == ND - 1) & (served < nsec - ND)
    served = lax.rem(served + nsec, nsec)
    onward = lax.rem(served + ND, nsec)
    via = (j == 0) & has_down
    via_from = lax.rem(jnp.where(place == 4, q + 3, q - 5) + nsec, nsec)

    barrier = pltpu.get_barrier_semaphore()
    met = jnp.int32(0)
    for cond, s, t in (
        (has_up, seg, up), (has_down, seg, down), (has_next, seg, nxt), (has_prev, seg, prv),
        (z_out, after, q), (z_in, before, q), (through, seg, relay), (relays, seg, served),
        (relays, seg, onward), (via, seg, via_from),
    ):
        @pl.when(cond)
        def _():
            pl.semaphore_signal(barrier, inc=1, device_id=(s, t), device_id_type=MESH)
        met = met + cond.astype(jnp.int32)

    def remote(src, dst, ss, rs, s, t):
        return pltpu.make_async_remote_copy(
            src_ref=src, dst_ref=dst, send_sem=ss, recv_sem=rs, device_id=(s, t), device_id_type=MESH)

    def rows_of(h):
        return pl.ds(pl.multiple_of(h * CHUNK, CHUNK), CHUNK)

    def e_copy():
        return remote(env_ref, prev1, e_ss, e_rs, seg, nxt)

    def b_copy(n):
        return remote(bm.at[n, pl.ds(2, 2)], bp.at[n], b_ss.at[n], b_rs.at[n], seg, nxt)

    def c1_copy(h):
        return remote(c1_snd.at[:, rows_of(h)], c1_in.at[:, rows_of(h)], c1_ss.at[h], c1_rs.at[h], seg, up)

    def rel_copy(h):
        return remote(c1_snd.at[:, rows_of(h)], rel.at[:, rows_of(h)], rel_ss.at[h], rel_rs.at[h], seg, relay)

    def fwd_copy(h):
        return remote(rel.at[:, rows_of(h)], c1_in.at[:, rows_of(h)], fwd_ss.at[h], c1_rs.at[h], seg, onward)

    def f_copy(h):
        return remote(env2.at[:, rows_of(h)], prev2.at[:, rows_of(h)], f_ss.at[h], f_rs.at[h], seg, nxt)

    def c2_copy(v):
        return remote(c2_snd.at[v], c2_in.at[v], c2_ss.at[v], c2_rs.at[v], seg, up)

    def z_copy(v):
        return remote(z_snd.at[v], out_ref.at[v], z_ss.at[v], z_rs.at[v], after, q)

    own = dims_ref[q]
    before_own = dims_ref[prv]
    row = lax.broadcasted_iota(jnp.int32, (cap, cap), 0)
    col = lax.broadcasted_iota(jnp.int32, (cap, cap), 1)

    def build_kron(n, states=range(4)):
        pick = lax.broadcasted_iota(jnp.int32, (span, wb), 0) // ROWS == lax.broadcasted_iota(jnp.int32, (span, wb), 1)
        pick = jnp.where(pick, 1.0, 0.0).astype(BF16)
        diag = (
            lax.rem(lax.broadcasted_iota(jnp.int32, (span, span), 0), ROWS)
            == lax.rem(lax.broadcasted_iota(jnp.int32, (span, span), 1), ROWS)
        )
        mpo = mpo_ref[n].astype(F32)
        for s in states:
            left = lax.dot_general(pick, mpo[:, s, :].astype(BF16), (((1,), (1,)), ((), ())), preferred_element_type=F32)
            both = lax.dot_general(left.astype(BF16), pick, (((1,), (1,)), ((), ())), preferred_element_type=F32)
            kron[n, pl.ds(s * span, span), :] = jnp.where(diag, both, 0.0).astype(BF16)

    def trim(n, s):
        ahead = (0, ND, 1, ND + 1)[s]
        ok = q + ahead < nsec
        if s >= 2:
            ok = ok & has_next
        width = dims_ref[jnp.where(ok, q + ahead, 0)] * ok.astype(jnp.int32) * mask_ref[n, s]
        b = blk_ref[n, s].astype(F32) * jnp.where((row < own) & (col < width), 1.0, 0.0)
        bm[n, s] = b.astype(BF16)
        if s == 0:
            to_a[n, :, pl.ds(0, cap)] = b.T.astype(BF16)
        if s == 1:
            to_c[n, :, pl.ds(0, cap)] = b.T.astype(BF16)

    def turn_prev(n):
        to_a[n, :, pl.ds(cap, cap)] = bp[n, 0].astype(F32).T.astype(BF16)
        to_c[n, :, pl.ds(cap, cap)] = bp[n, 1].astype(F32).T.astype(BF16)

    def front(n, h, source, first, blocks, limit, states):
        mixed = []
        for k in range(CHUNK // ROWS):
            rows = pl.ds(pl.multiple_of(h * CHUNK + k * ROWS, ROWS), ROWS)
            slab = source[:, rows, :]
            if limit is not None:
                slab = slab * live[limit, rows, :][None]
            weights = kron[n, pl.ds((2 * first + states[0]) * span, len(states) * span), :]
            mixed.append(dot(weights, slab.reshape(span, cap)).astype(BF16))
        for i, s in enumerate(states):
            half = (half_a, half_c)[s]
            stacked = jnp.concatenate([m[i * span:(i + 1) * span] for m in mixed], axis=0)
            got = dot(stacked, blocks[s]).astype(BF16)
            for k in range(CHUNK // ROWS):
                rows = pl.ds(pl.multiple_of(first * cap + h * CHUNK + k * ROWS, ROWS), ROWS)
                half[:, rows, :] = got[k * span:(k + 1) * span].reshape(wb, ROWS, cap)

    def front_own(n, h, states=(0, 1)):
        front(n, h, env2 if n else env_ref, 0, bm.at[n], None if n else 0, states)

    def front_prev(n, h, states=(0, 1)):
        front(n, h, prev2 if n else prev1, 1, bp.at[n], None if n else 1, states)

    build_kron(0, (1, 3))
    pl.semaphore_wait(barrier, met)

    @pl.when(has_next)
    def _():
        e_copy().start()

    trim(0, 2)
    trim(0, 3)

    @pl.when(has_next)
    def _():
        b_copy(0).start()

    trim(0, 1)
    live[0] = jnp.where((row < own) & (col < own), 1.0, 0.0).astype(BF16)
    each(pieces, 4, lambda h: front_own(0, h, (1,)))

    @pl.when(has_prev)
    def _():
        b_copy(0).wait_recv()
        live[1] = jnp.where((row < before_own) & (col < before_own), 1.0, 0.0).astype(BF16)
        turn_prev(0)
        e_copy().wait_recv()
        each(pieces, 4, lambda h: front_prev(0, h, (1,)))

    @pl.when(jnp.logical_not(has_prev))
    def _():
        half_c[:, pl.ds(cap, cap), :] = jnp.zeros((wb, cap, cap), BF16)
        for n in range(sites):
            to_c[n, :, pl.ds(cap, cap)] = jnp.zeros((cap, cap), BF16)

    @pl.when(has_up)
    def _():
        def one(v):
            c1_snd[v] = dot(to_c[0], half_c[v]).astype(BF16)
        each(wb, UNROLL, one)

        @pl.when(through)
        def _():
            each(RELAYED, 1, lambda h: rel_copy(h).start())
            each(pieces - RELAYED, 1, lambda h: c1_copy(h + RELAYED).start())

        @pl.when(jnp.logical_not(through))
        def _():
            each(pieces, 1, lambda h: c1_copy(h).start())

    @pl.when(jnp.logical_not(has_prev))
    def _():
        half_a[:, pl.ds(cap, cap), :] = jnp.zeros((wb, cap, cap), BF16)
        for n in range(sites):
            to_a[n, :, pl.ds(cap, cap)] = jnp.zeros((cap, cap), BF16)

    build_kron(0, (0, 2))
    trim(0, 0)
    for s in (2, 3, 0, 1):
        trim(1, s)

    @pl.when(has_next)
    def _():
        b_copy(1).start()

    build_kron(1)

    @pl.when(has_prev)
    def _():
        b_copy(1).wait_recv()
        turn_prev(1)

    each(pieces, 4, lambda h: front_own(0, h, (0,)))

    @pl.when(has_prev)
    def _():
        each(pieces, 4, lambda h: front_prev(0, h, (0,)))

    def keep(n):
        def one(v):
            acc[v] = dot(to_a[n], half_a[v])
        each(wb, UNROLL, one)

    keep(0)

    both = (j == 1) | (j == 2)

    def arrive(h):
        @pl.when(relays & (h + 2 < RELAYED))
        def _():
            rel_copy(h + 2).wait_recv()
            fwd_copy(h + 2).start()

        rows = rows_of(h)

        @pl.when(has_down)
        def _():
            c1_copy(h).wait_recv()
            env2[:, rows, :] = (acc[:, rows, :] + c1_in[:, rows, :].astype(F32)).astype(BF16)

        @pl.when(jnp.logical_not(has_down))
        def _():
            env2[:, rows, :] = acc[:, rows, :].astype(BF16)

        @pl.when(has_next)
        def _():
            f_copy(h).start()

        front_own(1, h)

        @pl.when(both & (h > 0))
        def _():
            f_copy(h - 1).wait_recv()
            front_prev(1, h - 1)

    @pl.when(relays)
    def _():
        def one(h):
            rel_copy(h).wait_recv()
            fwd_copy(h).start()
        each(2, 1, one)

    each(pieces, 1, arrive)

    @pl.when((q >= ND) & (q < 2 * ND))
    def _():
        pl.semaphore_signal(ready, inc=1, device_id=(seg, down), device_id_type=MESH)

    @pl.when(both)
    def _():
        f_copy(pieces - 1).wait_recv()
        front_prev(1, pieces - 1)

    @pl.when(j == ND - 1)
    def _():
        def one(h):
            f_copy(h).wait_recv()
            front_prev(1, h)
        each(pieces, 1, one)

    @pl.when(has_up)
    def _():
        @pl.when(q < ND)
        def _():
            pl.semaphore_wait(ready, 1)

        def one(v):
            c2_snd[v] = dot(to_c[1], half_c[v]).astype(BF16)
            c2_copy(v).start()
        each(wb, UNROLL, one)

    keep(1)

    def last(v):
        @pl.when(has_down)
        def _():
            c2_copy(v).wait_recv()
            acc[v] = acc[v] + c2_in[v].astype(F32)

        @pl.when(z_out)
        def _():
            z_snd[v] = acc[v].astype(BF16)
            z_copy(v).start()

    each(wb, 1, last)

    @pl.when(jnp.logical_not(z_in))
    def _():
        out_ref[...] = jnp.zeros_like(out_ref)

    @pl.when(has_next)
    def _():
        e_copy().wait_send()
        for n in range(sites):
            b_copy(n).wait_send()
        each(pieces, 1, lambda h: f_copy(h).wait_send())

    @pl.when(through)
    def _():
        each(RELAYED, 1, lambda h: rel_copy(h).wait_send())
        each(pieces - RELAYED, 1, lambda h: c1_copy(h + RELAYED).wait_send())

    @pl.when(has_up & jnp.logical_not(through))
    def _():
        each(pieces, 1, lambda h: c1_copy(h).wait_send())

    @pl.when(relays)
    def _():
        each(RELAYED, 1, lambda h: fwd_copy(h).wait_send())

    @pl.when(has_up)
    def _():
        each(wb, 1, lambda v: c2_copy(v).wait_send())

    @pl.when(z_out)
    def _():
        each(wb, 1, lambda v: z_copy(v).wait_send())

    @pl.when(z_in)
    def _():
        each(wb, 1, lambda v: z_copy(v).wait_recv())


def solution(mesh):
    nseg, nsec = mesh.shape["seg"], mesh.shape["sec"]

    def body(boundary_env, site_block_tensors, mpo_tensors, block_mask, sector_dims):
        env = boundary_env[0, 0]
        blocks = site_block_tensors[:, 0]
        masks = block_mask[:, 0]
        sites, wb, cap = blocks.shape[0], env.shape[0], env.shape[-1]
        span = wb * ROWS
        pieces = cap // CHUNK
        vmem = pl.BlockSpec(memory_space=pltpu.VMEM)
        smem = pl.BlockSpec(memory_space=pltpu.SMEM)
        whole = pltpu.VMEM((wb, cap, cap), BF16)
        half = pltpu.VMEM((wb, 2 * cap, cap), BF16)
        to = pltpu.VMEM((sites, cap, 2 * cap), BF16)
        one = pltpu.SemaphoreType.DMA
        by_site = pltpu.SemaphoreType.DMA((sites,))
        by_piece = pltpu.SemaphoreType.DMA((pieces,))
        by_channel = pltpu.SemaphoreType.DMA((wb,))
        out = pl.pallas_call(
            functools.partial(kernel, nseg, nsec),
            out_shape=jax.ShapeDtypeStruct(env.shape, BF16),
            in_specs=[vmem, vmem, vmem, smem, smem],
            out_specs=vmem,
            scratch_shapes=[
                pltpu.VMEM((sites, 4 * span, span), BF16),
                pltpu.VMEM((2, cap, cap), BF16),
                pltpu.VMEM((sites, 4, cap, cap), BF16),
                pltpu.VMEM((sites, 2, cap, cap), BF16),
                to, to, half, half,
                pltpu.VMEM((wb, cap, cap), F32),
                whole, whole, whole, whole, whole, whole, whole, whole, whole,
                one, one, by_site, by_site, by_piece, by_piece, by_piece, by_piece, by_piece, by_piece, by_piece,
                by_channel, by_channel, by_channel, by_channel,
                pltpu.SemaphoreType.REGULAR,
            ],
            compiler_params=pltpu.CompilerParams(
                collective_id=0, has_side_effects=True, vmem_limit_bytes=60 * 1024 * 1024),
        )(env, blocks, jnp.swapaxes(mpo_tensors, 1, 2), masks, sector_dims)
        return jnp.where(lax.axis_index("seg") > 0, out, 0)[None, None]

    in_specs = (
        P("seg", "sec", None, None, None),
        P("seg", "sec", None, None, None),
        P("seg", None, None, None),
        P("seg", "sec", None),
        P(),
    )
    return jax.shard_map(
        body, mesh=mesh, in_specs=in_specs, out_specs=P("seg", "sec", None, None, None), check_vma=False)
```

```python
import functools

import jax
import jax.numpy as jnp
from jax import lax
from jax.experimental import pallas as pl
from jax.experimental.pallas import tpu as pltpu
from jax.sharding import PartitionSpec as P

ND = 4
ROWS = 16
CHUNK = 32
RELAYED = 8
UNROLL = 4
MESH = pl.DeviceIdType.MESH
F32 = jnp.float32
BF16 = jnp.bfloat16


def dot(a, b):
    return jnp.dot(a, b, preferred_element_type=F32)


def each(count, step, body):
    def trip(k, carry):
        for u in range(step):
            body(k * step + u)
        return carry
    lax.fori_loop(0, count // step, trip, 0)
    for i in range(count // step * step, count):
        body(i)


def kernel(
    nseg, nsec,
    env_ref, blk_ref, mpo_ref, mask_ref, dims_ref,
    out_ref,
    kron, live, bm, bp, to_a, to_c, half_a, half_c, acc, prev1, env2, prev2, c1_snd, c1_in, rel, c2_snd, c2_in, z_snd,
    e_ss, e_rs, b_ss, b_rs, c1_ss, c1_rs, rel_ss, rel_rs, fwd_ss, f_ss, f_rs, c2_ss, c2_rs, z_ss, z_rs, ready,
):
    sites, wb, cap = blk_ref.shape[0], env_ref.shape[0], env_ref.shape[-1]
    span = wb * ROWS
    pieces = cap // CHUNK
    seg = lax.axis_index("seg")
    q = lax.axis_index("sec")
    j = lax.rem(q, ND)
    place = lax.rem(q, 2 * ND)
    has_up = q < nsec - ND
    has_down = q >= ND
    has_next = j < ND - 1
    has_prev = j > 0
    z_out = seg < nseg - 1
    z_in = seg > 0

    up = lax.rem(q + ND, nsec)
    down = lax.rem(q + nsec - ND, nsec)
    nxt = lax.rem(q + 1, nsec)
    prv = lax.rem(q + nsec - 1, nsec)
    after = lax.rem(seg + 1, nseg)
    before = lax.rem(seg + nseg - 1, nseg)

    through = (j == 0) & has_up
    relay = jnp.where(place == 0, q + 7, q - 1)
    relay = lax.rem(relay + nsec, nsec)
    served = jnp.where(place == 7, q - 7, q + 1)
    relays = (j == ND - 1) & (served < nsec - ND)
    served = lax.rem(served + nsec, nsec)
    onward = lax.rem(served + ND, nsec)
    via = (j == 0) & has_down
    via_from = lax.rem(jnp.where(place == 4, q + 3, q - 5) + nsec, nsec)

    barrier = pltpu.get_barrier_semaphore()
    met = jnp.int32(0)
    for cond, s, t in (
        (has_up, seg, up), (has_down, seg, down), (has_next, seg, nxt), (has_prev, seg, prv),
        (z_out, after, q), (z_in, before, q), (through, seg, relay), (relays, seg, served),
        (relays, seg, onward), (via, seg, via_from),
    ):
        @pl.when(cond)
        def _():
            pl.semaphore_signal(barrier, inc=1, device_id=(s, t), device_id_type=MESH)
        met = met + cond.astype(jnp.int32)

    def remote(src, dst, ss, rs, s, t):
        return pltpu.make_async_remote_copy(
            src_ref=src, dst_ref=dst, send_sem=ss, recv_sem=rs, device_id=(s, t), device_id_type=MESH)

    def rows_of(h):
        return pl.ds(pl.multiple_of(h * CHUNK, CHUNK), CHUNK)

    def e_copy():
        return remote(env_ref, prev1, e_ss, e_rs, seg, nxt)

    def b_copy(n):
        return remote(bm.at[n, pl.ds(2, 2)], bp.at[n], b_ss.at[n], b_rs.at[n], seg, nxt)

    def c1_copy(h):
        return remote(c1_snd.at[:, rows_of(h)], c1_in.at[:, rows_of(h)], c1_ss.at[h], c1_rs.at[h], seg, up)

    def rel_copy(h):
        return remote(c1_snd.at[:, rows_of(h)], rel.at[:, rows_of(h)], rel_ss.at[h], rel_rs.at[h], seg, relay)

    def fwd_copy(h):
        return remote(rel.at[:, rows_of(h)], c1_in.at[:, rows_of(h)], fwd_ss.at[h], c1_rs.at[h], seg, onward)

    def f_copy(h):
        return remote(env2.at[:, rows_of(h)], prev2.at[:, rows_of(h)], f_ss.at[h], f_rs.at[h], seg, nxt)

    def c2_copy(v):
        return remote(c2_snd.at[v], c2_in.at[v], c2_ss.at[v], c2_rs.at[v], seg, up)

    def z_copy(v):
        return remote(z_snd.at[v], out_ref.at[v], z_ss.at[v], z_rs.at[v], after, q)

    own = dims_ref[q]
    before_own = dims_ref[prv]
    row = lax.broadcasted_iota(jnp.int32, (cap, cap), 0)
    col = lax.broadcasted_iota(jnp.int32, (cap, cap), 1)

    def build_kron(n, states=range(4)):
        pick = lax.broadcasted_iota(jnp.int32, (span, wb), 0) // ROWS == lax.broadcasted_iota(jnp.int32, (span, wb), 1)
        pick = jnp.where(pick, 1.0, 0.0).astype(BF16)
        diag = (
            lax.rem(lax.broadcasted_iota(jnp.int32, (span, span), 0), ROWS)
            == lax.rem(lax.broadcasted_iota(jnp.int32, (span, span), 1), ROWS)
        )
        mpo = mpo_ref[n].astype(F32)
        for s in states:
            left = lax.dot_general(pick, mpo[:, s, :].astype(BF16), (((1,), (1,)), ((), ())), preferred_element_type=F32)
            both = lax.dot_general(left.astype(BF16), pick, (((1,), (1,)), ((), ())), preferred_element_type=F32)
            kron[n, pl.ds(s * span, span), :] = jnp.where(diag, both, 0.0).astype(BF16)

    def trim(n, s):
        ahead = (0, ND, 1, ND + 1)[s]
        ok = q + ahead < nsec
        if s >= 2:
            ok = ok & has_next
        width = dims_ref[jnp.where(ok, q + ahead, 0)] * ok.astype(jnp.int32) * mask_ref[n, s]
        b = blk_ref[n, s].astype(F32) * jnp.where((row < own) & (col < width), 1.0, 0.0)
        bm[n, s] = b.astype(BF16)
        if s == 0:
            to_a[n, :, pl.ds(0, cap)] = b.T.astype(BF16)
        if s == 1:
            to_c[n, :, pl.ds(0, cap)] = b.T.astype(BF16)

    def turn_prev(n):
        to_a[n, :, pl.ds(cap, cap)] = bp[n, 0].astype(F32).T.astype(BF16)
        to_c[n, :, pl.ds(cap, cap)] = bp[n, 1].astype(F32).T.astype(BF16)

    def front(n, h, source, first, blocks, limit, states):
        mixed = []
        for k in range(CHUNK // ROWS):
            rows = pl.ds(pl.multiple_of(h * CHUNK + k * ROWS, ROWS), ROWS)
            slab = source[:, rows, :]
            if limit is not None:
                slab = slab * live[limit, rows, :][None]
            weights = kron[n, pl.ds((2 * first + states[0]) * span, len(states) * span), :]
            mixed.append(dot(weights, slab.reshape(span, cap)).astype(BF16))
        for i, s in enumerate(states):
            half = (half_a, half_c)[s]
            stacked = jnp.concatenate([m[i * span:(i + 1) * span] for m in mixed], axis=0)
            got = dot(stacked, blocks[s]).astype(BF16)
            for k in range(CHUNK // ROWS):
                rows = pl.ds(pl.multiple_of(first * cap + h * CHUNK + k * ROWS, ROWS), ROWS)
                half[:, rows, :] = got[k * span:(k + 1) * span].reshape(wb, ROWS, cap)

    def front_own(n, h, states=(0, 1)):
        front(n, h, env2 if n else env_ref, 0, bm.at[n], None if n else 0, states)

    def front_prev(n, h, states=(0, 1)):
        front(n, h, prev2 if n else prev1, 1, bp.at[n], None if n else 1, states)

    build_kron(0, (1, 3))
    pl.semaphore_wait(barrier, met)

    @pl.when(has_next)
    def _():
        e_copy().start()

    trim(0, 2)
    trim(0, 3)

    @pl.when(has_next)
    def _():
        b_copy(0).start()

    trim(0, 1)
    live[0] = jnp.where((row < own) & (col < own), 1.0, 0.0).astype(BF16)
    each(pieces, 4, lambda h: front_own(0, h, (1,)))

    @pl.when(has_prev)
    def _():
        b_copy(0).wait_recv()
        live[1] = jnp.where((row < before_own) & (col < before_own), 1.0, 0.0).astype(BF16)
        turn_prev(0)
        e_copy().wait_recv()
        each(pieces, 4, lambda h: front_prev(0, h, (1,)))

    @pl.when(jnp.logical_not(has_prev))
    def _():
        half_c[:, pl.ds(cap, cap), :] = jnp.zeros((wb, cap, cap), BF16)
        for n in range(sites):
            to_c[n, :, pl.ds(cap, cap)] = jnp.zeros((cap, cap), BF16)

    @pl.when(has_up)
    def _():
        def one(v):
            c1_snd[v] = dot(to_c[0], half_c[v]).astype(BF16)
        each(wb, UNROLL, one)

        @pl.when(through)
        def _():
            each(RELAYED, 1, lambda h: rel_copy(h).start())
            each(pieces - RELAYED, 1, lambda h: c1_copy(h + RELAYED).start())

        @pl.when(jnp.logical_not(through))
        def _():
            each(pieces, 1, lambda h: c1_copy(h).start())

    @pl.when(jnp.logical_not(has_prev))
    def _():
        half_a[:, pl.ds(cap, cap), :] = jnp.zeros((wb, cap, cap), BF16)
        for n in range(sites):
            to_a[n, :, pl.ds(cap, cap)] = jnp.zeros((cap, cap), BF16)

    build_kron(0, (0, 2))
    trim(0, 0)
    for s in (2, 3, 0, 1):
        trim(1, s)

    build_kron(1)

    each(pieces, 4, lambda h: front_own(0, h, (0,)))

    @pl.when(has_prev)
    def _():
        each(pieces, 4, lambda h: front_prev(0, h, (0,)))

    def keep(n):
        def one(v):
            acc[v] = dot(to_a[n], half_a[v])
        each(wb, UNROLL, one)

    keep(0)

    @pl.when(has_next)
    def _():
        b_copy(1).start()

    @pl.when(has_prev)
    def _():
        b_copy(1).wait_recv()
        turn_prev(1)

    both = (j == 1) | (j == 2)

    def arrive(h):
        @pl.when(relays & (h + 4 < RELAYED))
        def _():
            rel_copy(h + 4).wait_recv()
            fwd_copy(h + 4).start()

        rows = rows_of(h)

        @pl.when(has_down)
        def _():
            c1_copy(h).wait_recv()
            env2[:, rows, :] = (acc[:, rows, :] + c1_in[:, rows, :].astype(F32)).astype(BF16)

        @pl.when(jnp.logical_not(has_down))
        def _():
            env2[:, rows, :] = acc[:, rows, :].astype(BF16)

        @pl.when(has_next)
        def _():
            f_copy(h).start()

        front_own(1, h)

        @pl.when(both & (h > 0))
        def _():
            f_copy(h - 1).wait_recv()
            front_prev(1, h - 1)

    @pl.when(relays)
    def _():
        def one(h):
            rel_copy(h).wait_recv()
            fwd_copy(h).start()
        each(4, 1, one)

    each(pieces, 1, arrive)

    @pl.when((q >= ND) & (q < 2 * ND))
    def _():
        pl.semaphore_signal(ready, inc=1, device_id=(seg, down), device_id_type=MESH)

    @pl.when(both)
    def _():
        f_copy(pieces - 1).wait_recv()
        front_prev(1, pieces - 1)

    @pl.when(j == ND - 1)
    def _():
        def one(h):
            f_copy(h).wait_recv()
            front_prev(1, h)
        each(pieces, 1, one)

    @pl.when(has_up)
    def _():
        @pl.when(q < ND)
        def _():
            pl.semaphore_wait(ready, 1)

        def one(v):
            c2_snd[v] = dot(to_c[1], half_c[v]).astype(BF16)
            c2_copy(v).start()
        each(wb, UNROLL, one)

    keep(1)

    def last(v):
        @pl.when(has_down)
        def _():
            c2_copy(v).wait_recv()
            acc[v] = acc[v] + c2_in[v].astype(F32)

        @pl.when(z_out)
        def _():
            z_snd[v] = acc[v].astype(BF16)
            z_copy(v).start()

    each(wb, 1, last)

    @pl.when(jnp.logical_not(z_in))
    def _():
        out_ref[...] = jnp.zeros_like(out_ref)

    @pl.when(has_next)
    def _():
        e_copy().wait_send()
        for n in range(sites):
            b_copy(n).wait_send()
        each(pieces, 1, lambda h: f_copy(h).wait_send())

    @pl.when(through)
    def _():
        each(RELAYED, 1, lambda h: rel_copy(h).wait_send())
        each(pieces - RELAYED, 1, lambda h: c1_copy(h + RELAYED).wait_send())

    @pl.when(has_up & jnp.logical_not(through))
    def _():
        each(pieces, 1, lambda h: c1_copy(h).wait_send())

    @pl.when(relays)
    def _():
        each(RELAYED, 1, lambda h: fwd_copy(h).wait_send())

    @pl.when(has_up)
    def _():
        each(wb, 1, lambda v: c2_copy(v).wait_send())

    @pl.when(z_out)
    def _():
        each(wb, 1, lambda v: z_copy(v).wait_send())

    @pl.when(z_in)
    def _():
        each(wb, 1, lambda v: z_copy(v).wait_recv())


def solution(mesh):
    nseg, nsec = mesh.shape["seg"], mesh.shape["sec"]

    def body(boundary_env, site_block_tensors, mpo_tensors, block_mask, sector_dims):
        env = boundary_env[0, 0]
        blocks = site_block_tensors[:, 0]
        masks = block_mask[:, 0]
        sites, wb, cap = blocks.shape[0], env.shape[0], env.shape[-1]
        span = wb * ROWS
        pieces = cap // CHUNK
        vmem = pl.BlockSpec(memory_space=pltpu.VMEM)
        smem = pl.BlockSpec(memory_space=pltpu.SMEM)
        whole = pltpu.VMEM((wb, cap, cap), BF16)
        half = pltpu.VMEM((wb, 2 * cap, cap), BF16)
        to = pltpu.VMEM((sites, cap, 2 * cap), BF16)
        one = pltpu.SemaphoreType.DMA
        by_site = pltpu.SemaphoreType.DMA((sites,))
        by_piece = pltpu.SemaphoreType.DMA((pieces,))
        by_channel = pltpu.SemaphoreType.DMA((wb,))
        out = pl.pallas_call(
            functools.partial(kernel, nseg, nsec),
            out_shape=jax.ShapeDtypeStruct(env.shape, BF16),
            in_specs=[vmem, vmem, vmem, smem, smem],
            out_specs=vmem,
            scratch_shapes=[
                pltpu.VMEM((sites, 4 * span, span), BF16),
                pltpu.VMEM((2, cap, cap), BF16),
                pltpu.VMEM((sites, 4, cap, cap), BF16),
                pltpu.VMEM((sites, 2, cap, cap), BF16),
                to, to, half, half,
                pltpu.VMEM((wb, cap, cap), F32),
                whole, whole, whole, whole, whole, whole, whole, whole, whole,
                one, one, by_site, by_site, by_piece, by_piece, by_piece, by_piece, by_piece, by_piece, by_piece,
                by_channel, by_channel, by_channel, by_channel,
                pltpu.SemaphoreType.REGULAR,
            ],
            compiler_params=pltpu.CompilerParams(
                collective_id=0, has_side_effects=True, vmem_limit_bytes=60 * 1024 * 1024),
        )(env, blocks, jnp.swapaxes(mpo_tensors, 1, 2), masks, sector_dims)
        return jnp.where(lax.axis_index("seg") > 0, out, 0)[None, None]

    in_specs = (
        P("seg", "sec", None, None, None),
        P("seg", "sec", None, None, None),
        P("seg", None, None, None),
        P("seg", "sec", None),
        P(),
    )
    return jax.shard_map(
        body, mesh=mesh, in_specs=in_specs, out_specs=P("seg", "sec", None, None, None), check_vma=False)
```
